256 devices in a mesh: ctx: 16 (over z, core), head: 16 (over x, y).
Axes of the slice: x: 4, y: 4, z: 8, core: 2. Of those that a mesh axis runs over, the one named last changes fastest.
Arguments:
- queries: float32 [24576, 16, 4, 128], P(('ctx', 'head')), may hold values from -6 to 6
- key_vectors: float32 [24576, 16, 4, 128], P(('ctx', 'head')), may hold values from -0.6 to 0.6
- value_vectors: float32 [24576, 16, 4, 128], P(('ctx', 'head')), may hold values from -6 to 6
- log_decay: float32 [24576, 16, 4], P(('ctx', 'head')), may hold values from -1.5 to 0
- doc_lengths: int32 [16], replicated, may hold values from 1 to 6144, 24576 in all
Outputs:
- lightning_out: float32 [24576, 64, 128], P('ctx', 'head')
The draws below stay inside these ranges and needn't reach their ends.
Inputs may be any that keep to these rules, and one draw needn't show every extreme that they name: `doc_lengths`: the 16 documents lie end to end and fill all 24576 tokens; the longest has exactly 6144 tokens.
All inputs are finite; a program needn't handle non-finite values.
Results may differ from the reference program's by a relative error of at most 0.0003.
Values sent between devices are 32-bit elements; how exact they have to be, the bound alone decides.
A program may use at most 128 MiB of HBM per device.

```python
import math
from functools import partial
import jax
import jax.numpy as jnp
import numpy as np
from jax import lax

HEAD_TOTAL = 64
DH = 128
NDOC = 16
TOKEN_TOTAL = 24576
N_HEAD = 16


def draw_log_decay(key, part):
    decay_random_key, select_random_key, quick_random_key, noise_random_key, position_random_key, surge_random_key = jax.random.split(jax.random.fold_in(key, 17), 6)
    fast_share = 0.5
    slow_rate = jnp.exp(jax.random.uniform(decay_random_key, (HEAD_TOTAL,), jnp.float32, math.log(0.05 / TOKEN_TOTAL), math.log(0.5 / TOKEN_TOTAL)))
    fast_rate = jax.random.uniform(quick_random_key, (HEAD_TOTAL,), jnp.float32, 1.0 / 50.0, 1.0 / 30.0)
    is_fast = jax.random.uniform(select_random_key, (HEAD_TOTAL,), jnp.float32) < fast_share
    base_rate = jnp.where(is_fast, fast_rate, slow_rate)
    jitter = jax.random.uniform(noise_random_key, (TOKEN_TOTAL, HEAD_TOTAL), jnp.float32, 0.5, 1.5)
    gate_logarithms = -base_rate[None, :] * jitter
    surge_positions = jax.random.randint(position_random_key, (3, HEAD_TOTAL), 0, TOKEN_TOTAL)
    surge_length = jnp.log(jax.random.uniform(surge_random_key, (3, HEAD_TOTAL), jnp.float32, 0.5, 0.8))
    current_head = jnp.broadcast_to(jnp.arange(HEAD_TOTAL, dtype=jnp.int32)[None, :], (3, HEAD_TOTAL))
    gate_logarithms = gate_logarithms.at[surge_positions, current_head].add(surge_length)
    return gate_logarithms.reshape(TOKEN_TOTAL, N_HEAD, HEAD_TOTAL // N_HEAD)


def block_levels(stream_key, shape, pieces, least, high):
    factor_of, own = 1.0, jax.random.fold_in(stream_key, 6)
    for axis_at, shards_of in pieces:
        steps = jnp.exp(jax.random.uniform(jax.random.fold_in(own, axis_at), (shards_of,), jnp.float32, least / len(pieces), high / len(pieces)))
        factor_of = factor_of * jnp.repeat(steps, shape[axis_at] // shards_of).reshape([-1 if axis == axis_at else 1 for axis in range(len(shape))])
    return factor_of


def length_profile(number_of, total, reach, skew):
    portions = [(1 << 20) // math.isqrt(grade ** skew) + 1 for grade in range(2, number_of + 1)]
    surplus, given = total - reach - (number_of - 1), [1] * (number_of - 1)
    while surplus > 0:
        candidates = [i for i in range(number_of - 1) if given[i] < reach]
        whole, left = sum([portions[i] for i in candidates]), surplus
        for i in candidates:
            more = min(reach - given[i], max(1, left * portions[i] // whole), surplus)
            given[i] = given[i] + more
            surplus = surplus - more
    return np.array([reach] + given)


def ragged(stream_key, count, total, limit, skew):
    if count == 2:
        one = jax.random.randint(stream_key, (), max(1, total - limit), min(limit, total - 1) + 1)
        return jnp.stack([one, total - one])
    sizes = jnp.asarray(length_profile(count, total, limit, skew), jnp.int32)
    twos = (count - 1) // 2
    donor, sink = sizes[1:1 + 2 * twos:2], sizes[2:2 + 2 * twos:2]
    slack = jnp.minimum(donor - 1, limit - sink)
    shifted = jax.random.randint(jax.random.fold_in(stream_key, 1), (twos,), 0, 1 << 20) % (slack + 1)
    sizes = sizes.at[1:1 + 2 * twos:2].set(donor - shifted).at[2:2 + 2 * twos:2].set(sink + shifted)
    return sizes[jax.random.permutation(jax.random.fold_in(stream_key, 2), count)]


def bell_draw(stream_key, extent, width, bound, pieces=(), kind=jnp.bfloat16):
    factor_of = block_levels(stream_key, extent, pieces, -0.22, 0.18) if pieces else 1.0
    drawn = jax.random.normal(stream_key, extent, jnp.float32) * width * factor_of
    return jnp.minimum(jnp.maximum(drawn, -bound), bound).astype(kind)


def setup_inputs(seed: int = 0) -> dict:
    key_list = jax.random.split(jax.random.key(seed), 6)
    queries = bell_draw(key_list[0], (TOKEN_TOTAL, N_HEAD, HEAD_TOTAL // N_HEAD, DH), 1.0, 6.0, ((0, 256),), jnp.float32)
    key_vectors = bell_draw(key_list[1], (TOKEN_TOTAL, N_HEAD, HEAD_TOTAL // N_HEAD, DH), 0.1, 0.6, ((0, 256),), jnp.float32)
    value_vectors = bell_draw(key_list[2], (TOKEN_TOTAL, N_HEAD, HEAD_TOTAL // N_HEAD, DH), 1.0, 6.0, ((0, 256),), jnp.float32)
    log_decay = draw_log_decay(jax.random.fold_in(key_list[5], 71), 0)
    doc_lengths = ragged(key_list[4], NDOC, TOKEN_TOTAL, TOKEN_TOTAL // 4, 2).astype(jnp.int32)
    return dict(queries=queries, key_vectors=key_vectors, value_vectors=value_vectors, log_decay=log_decay, doc_lengths=doc_lengths)


PRECISE = lax.Precision.HIGHEST
EPSILON = 1e-06

def block_step(carry_in, block_in, want_out):
    state, factor = carry_in
    query_rows, key_rows, value_rows, gate_rows, doc_ids, prev_doc = block_in
    block_len = doc_ids.shape[0]
    cumulative = jnp.cumsum(gate_rows, axis=0)
    row_index = lax.broadcasted_iota(jnp.int32, (block_len, block_len), 0)
    col_index = lax.broadcasted_iota(jnp.int32, (block_len, block_len), 1)
    visible = (row_index >= col_index) & (doc_ids[:, None] == doc_ids[None, :])
    heads_cum = jnp.transpose(cumulative)
    exponent = heads_cum[:, :, None] - heads_cum[:, None, :]
    weights = jnp.where(visible[None], jnp.exp(jnp.where(visible[None], exponent, 0.0)), 0.0)
    carry_coef = jnp.where((doc_ids == prev_doc)[:, None], jnp.exp(cumulative), 0.0)
    tail_coef = jnp.where((doc_ids == doc_ids[block_len - 1])[:, None], jnp.exp(cumulative[block_len - 1][None, :] - cumulative), 0.0)
    new_state = jnp.einsum('shd,she->hde', key_rows * tail_coef[:, :, None], value_rows, precision=PRECISE) + carry_coef[block_len - 1][:, None, None] * state
    new_factor = carry_coef[block_len - 1] * factor
    if want_out:
        scores = jnp.einsum('thd,shd->hts', query_rows, key_rows, precision=PRECISE) * weights
        local_out = jnp.einsum('hts,shd->thd', scores, value_rows, precision=PRECISE)
        carried = jnp.einsum('thd,hde->the', query_rows, state, precision=PRECISE)
        return ((new_state, new_factor), (local_out + carry_coef[:, :, None] * carried, carry_coef * factor[None, :]))
    return ((new_state, new_factor), None)

def reference(queries, key_vectors, value_vectors, log_decay, doc_lengths):
    block_len = min(512, TOKEN_TOTAL)
    block_count = TOKEN_TOTAL // block_len
    query_all = queries.reshape(block_count, block_len, HEAD_TOTAL, DH)
    key_all = key_vectors.reshape(block_count, block_len, HEAD_TOTAL, DH)
    value_all = value_vectors.reshape(block_count, block_len, HEAD_TOTAL, DH)
    gate_all = log_decay.reshape(block_count, block_len, HEAD_TOTAL)
    positions = lax.iota(jnp.int32, TOKEN_TOTAL)
    doc_ends = jnp.cumsum(doc_lengths).astype(jnp.int32)
    doc_ids = lax.optimization_barrier(jnp.sum((doc_ends[None, :] <= positions[:, None]).astype(jnp.int32), axis=1)).astype(jnp.int32)
    block_docs = doc_ids.reshape(block_count, block_len)
    prev_docs = jnp.concatenate([jnp.full((1,), -1, jnp.int32), block_docs[:-1, block_len - 1].astype(jnp.int32)])
    start_carry = (jnp.zeros((HEAD_TOTAL, DH, DH), queries.dtype), jnp.ones((HEAD_TOTAL,), queries.dtype))
    blocked = (query_all, key_all, value_all, gate_all, block_docs, prev_docs)
    unused, outputs = lax.scan(partial(block_step, want_out=True), start_carry, blocked)
    mixed_rows = outputs[0].reshape(TOKEN_TOTAL, HEAD_TOTAL, DH)
    return mixed_rows * lax.rsqrt(lax.optimization_barrier(jnp.mean(mixed_rows * mixed_rows, axis=-1, keepdims=True)) + EPSILON)
```

```python
import functools

import jax
import jax.numpy as jnp
from jax import lax
from jax.experimental import pallas as pl
from jax.experimental.pallas import tpu as pltpu
from jax.sharding import PartitionSpec as P

EPSILON = 1e-06
SIDE = 4
BLOCKED = -1e30
EXACT = lax.Precision.HIGHEST
MESH = pl.DeviceIdType.MESH

GROUPS = ((1, 3, 4, 12), (5, 15, 7, 13), (2, 8), (6, 14, 9, 11), (10,))
ORDER = (0,) + sum(GROUPS, ())
FIRST_CODES = sum(off << (4 * n) for n, off in enumerate(ORDER[:8]))
LAST_CODES = sum(off << (4 * n) for n, off in enumerate(ORDER[8:])) - (1 << 32)


def split(x):
    high = x.astype(jnp.bfloat16)
    return high, (x - high.astype(jnp.float32)).astype(jnp.bfloat16)


def twice(high, low):
    row = jnp.concatenate([high, low], axis=1)
    return jnp.concatenate([row, row], axis=0)


def stacked(high, low):
    return jnp.concatenate(
        [jnp.concatenate([high, high], axis=1), jnp.concatenate([low, low], axis=1)],
        axis=0,
    )


def halves(x):
    half = x.shape[1] // 2
    return x[:, :half] + x[:, half:]


def product(left, right):
    return halves(jnp.dot(left, right, preferred_element_type=jnp.float32))


def product_t(left, right):
    return halves(
        lax.dot_general(
            left, right, (((1,), (1,)), ((), ())), preferred_element_type=jnp.float32
        )
    )


def kernel(
    tokens, heads, n_ctx,
    docs, q, k, v, gates, out,
    land, gate_in, keep, tail, carry, step, update,
    k_high, k_low, v_high, v_low, s_high, s_low, own_state, near_states, near_sum, far_sum, rows_out,
    send_sem, recv_sem, gate_send, gate_recv, state_send, state_recv, out_sem,
):
    sources = SIDE * SIDE
    wide = 128
    ctx = lax.axis_index("ctx")
    me = lax.axis_index("head")
    x, y = me // SIDE, me % SIDE

    def to(off):
        return (x + off // SIDE) % SIDE * SIDE + (y + off % SIDE) % SIDE

    def source(n):
        codes = jnp.where(n < 8, FIRST_CODES, LAST_CODES)
        off = lax.shift_right_arithmetic(codes, 4 * (n % 8)) % 16
        return (x + SIDE - off // SIDE) % SIDE * SIDE + (y + SIDE - off % SIDE) % SIDE

    arrays = (k, v, q)
    K, V, Q = range(3)

    for a, array in enumerate(arrays):
        for j in range(heads):
            pltpu.make_async_copy(
                array.at[:, me, j], land.at[a, me, j], recv_sem.at[a, me]
            ).start()
    pltpu.make_async_copy(gates.at[me], gate_in.at[me], gate_recv.at[me]).start()

    barrier = pltpu.get_barrier_semaphore()
    for off in range(1, sources):
        pl.semaphore_signal(barrier, inc=1, device_id={"head": to(off)}, device_id_type=MESH)
    for hop in (1, 2, n_ctx - 1, n_ctx - 2):
        pl.semaphore_signal(
            barrier, inc=1, device_id={"ctx": (ctx + hop) % n_ctx}, device_id_type=MESH
        )
    pl.semaphore_wait(barrier, sources + 3)

    for off in ORDER[1:]:
        pltpu.make_async_remote_copy(
            src_ref=gates.at[to(off)], dst_ref=gate_in.at[me],
            send_sem=gate_send, recv_sem=gate_recv.at[me],
            device_id={"head": to(off)}, device_id_type=MESH,
        ).start()
    for a, array in enumerate(arrays):
        for group in GROUPS:
            for j in range(heads):
                for off in group:
                    pltpu.make_async_remote_copy(
                        src_ref=array.at[:, to(off), j], dst_ref=land.at[a, me, j],
                        send_sem=send_sem.at[a], recv_sem=recv_sem.at[a, me],
                        device_id={"head": to(off)}, device_id_type=MESH,
                    ).start()

    for ref in (k_high, k_low, v_high, v_low):

        def clear(s, _, ref=ref):
            for j in range(heads):
                ref[s, j, tokens:, :] = jnp.zeros((wide - tokens, wide), jnp.bfloat16)
            return 0

        lax.fori_loop(0, sources, clear, 0)
    ends = []
    for d in range(docs.shape[0]):
        ends.append(docs[d] + (ends[-1] if ends else 0))

    def doc_of(position):
        return sum((end <= position).astype(jnp.int32) for end in ends)

    row = lax.broadcasted_iota(jnp.int32, (tokens, wide), 0)
    col = lax.broadcasted_iota(jnp.int32, (tokens, wide), 1)
    upto_col = (row <= col).astype(jnp.float32)
    upto_row = (row >= col).astype(jnp.float32)[:, :tokens]

    def weigh(s, _):
        pltpu.make_async_copy(gate_in.at[s], gate_in.at[s], gate_recv.at[s]).wait()
        gate = gate_in[s]
        along_row = jnp.dot(gate, upto_col, precision=EXACT, preferred_element_type=jnp.float32)
        along_col = lax.dot_general(
            upto_row, gate, (((1,), (1,)), ((), ())), precision=EXACT, preferred_element_type=jnp.float32
        )
        start = (ctx * sources + s) * tokens
        doc_col = doc_of(start + row)
        doc_row = doc_of(start + col[:1])
        before = jnp.full((1, wide), start - 1, jnp.int32)
        doc_before = jnp.where(before >= 0, doc_of(before), -1)
        doc_last = doc_of(before + tokens)
        seen = (row >= col) & (doc_col == doc_row)
        same_first = doc_col == doc_before
        same_last = doc_col == doc_last
        for j in range(heads):
            col_sum = jnp.broadcast_to(along_col[:, j : j + 1], (tokens, wide))
            row_sum = along_row[j : j + 1, :]
            last = along_row[j : j + 1, tokens - 1 : tokens]
            keep[s, j] = jnp.exp(jnp.where(seen, col_sum - row_sum, BLOCKED))
            tail[s, j] = jnp.exp(jnp.where(same_last, last - col_sum, BLOCKED))
            through = jnp.exp(jnp.where(same_first, col_sum, BLOCKED))
            carry[s, j] = through
            step[s, j] = jnp.broadcast_to(through[tokens - 1 :, :], (8, wide))
        return 0

    lax.fori_loop(0, sources, weigh, 0)

    def arrived(a, s):
        pltpu.make_async_copy(land.at[a, s], land.at[a, s], recv_sem.at[a, s]).wait()

    filler = jnp.zeros((wide - tokens, wide), jnp.float32)

    def gather(n, _):
        s = source(n)
        arrived(K, s)
        arrived(V, s)
        for j in range(heads):
            keys = land[K, s, j]
            values = land[V, s, j]
            k_high[s, j, :tokens, :], k_low[s, j, :tokens, :] = split(keys)
            v_high[s, j, :tokens, :], v_low[s, j, :tokens, :] = split(values)
            weighted = jnp.concatenate([keys * tail[s, j], filler], axis=0)
            flipped = jnp.concatenate([values, filler], axis=0).T
            update[s, j] = product(
                jnp.concatenate(split(flipped), axis=1), twice(*split(weighted))
            )
        return 0

    lax.fori_loop(0, sources, gather, 0)

    for j in range(heads):

        def onward(s, running, j=j):
            state, factor = running
            return step[s, j, :1, :] * state + update[s, j], step[s, j] * factor

        state, factor = lax.fori_loop(
            0, sources, onward, (jnp.zeros((wide, wide), jnp.float32), jnp.ones((8, wide), jnp.float32))
        )
        own_state[j, :wide, :] = state
        own_state[j, wide:, :] = factor

    def pass_on(source_ref, target_ref, n, hop):
        return pltpu.make_async_remote_copy(
            src_ref=source_ref, dst_ref=target_ref, send_sem=state_send.at[n], recv_sem=state_recv.at[n],
            device_id={"ctx": (ctx + hop) % n_ctx}, device_id_type=MESH,
        )

    by_one = pass_on(own_state, near_states.at[0], 0, 1)
    by_two = pass_on(own_state, near_states.at[1], 1, 2)
    sums = pass_on(near_sum, far_sum, 2, 2)
    by_two.start()
    by_one.start()
    by_one.wait_recv()
    by_two.wait_recv()
    for j in range(heads):
        near_sum[j] = near_states[0, j, :wide, :] + near_states[0, j, wide : wide + 1, :] * near_states[1, j, :wide, :]
    sums.start()
    sums.wait_recv()

    for j in range(heads):
        both = near_states[0, j, wide : wide + 1, :] * near_states[1, j, wide : wide + 1, :]

        def enter(s, state, j=j):
            s_high[s, j], s_low[s, j] = split(state)
            return step[s, j, :1, :] * state + update[s, j]

        lax.fori_loop(0, sources, enter, near_sum[j] + both * far_sum[j])

    def answer(n, _):
        s = source(n)
        arrived(Q, s)
        for j in range(heads):
            queries = jnp.concatenate(split(land[Q, s, j]), axis=1)
            scores = product_t(queries, stacked(k_high[s, j], k_low[s, j]))
            carried = product_t(queries, stacked(s_high[s, j], s_low[s, j]))
            weights = jnp.concatenate(split(scores * keep[s, j]), axis=1)
            mixed = product(weights, twice(v_high[s, j], v_low[s, j])) + carry[s, j] * carried
            size = jnp.mean(mixed * mixed, axis=1, keepdims=True)
            rows_out[pl.ds(s * (tokens * heads) + j, tokens, stride=heads), :] = mixed * lax.rsqrt(size + EPSILON)
        pltpu.make_async_copy(
            rows_out.at[pl.ds(s * (tokens * heads), tokens * heads)].reshape(tokens, heads, wide),
            out.at[pl.ds(s * tokens, tokens)],
            out_sem,
        ).start()
        return 0

    lax.fori_loop(0, sources, answer, 0)

    by_one.wait_send()
    by_two.wait_send()
    sums.wait_send()
    others = pl.ds(0, sources - 1)
    pltpu.make_async_copy(gates.at[others], gates.at[others], gate_send).wait()
    for a, array in enumerate(arrays):
        pltpu.make_async_copy(array.at[:, others], array.at[:, others], send_sem.at[a]).wait()
    pltpu.make_async_copy(out, out, out_sem).wait()


def per_device(n_ctx, queries, key_vectors, value_vectors, log_decay, doc_lengths):
    tokens, sources, heads, wide = queries.shape
    f32 = jnp.float32
    hbm = pl.BlockSpec(memory_space=pl.ANY)
    per_block = (sources, heads)
    block = pltpu.VMEM((*per_block, tokens, wide), f32)
    square = pltpu.VMEM((*per_block, wide, wide), jnp.bfloat16)
    states = pltpu.VMEM((heads, wide, wide), f32)
    total = tokens * sources
    return pl.pallas_call(
        functools.partial(kernel, tokens, heads, n_ctx),
        out_shape=jax.ShapeDtypeStruct((total, heads, wide), f32),
        in_specs=[pl.BlockSpec(memory_space=pltpu.SMEM), hbm, hbm, hbm, hbm],
        out_specs=hbm,
        scratch_shapes=[
            pltpu.VMEM((3, *per_block, tokens, wide), f32),
            pltpu.VMEM((sources, heads, tokens), f32),
            block,
            block,
            block,
            pltpu.VMEM((*per_block, 8, wide), f32),
            pltpu.VMEM((*per_block, wide, wide), f32),
            *[square] * 6,
            pltpu.VMEM((heads, wide + 8, wide), f32),
            pltpu.VMEM((2, heads, wide + 8, wide), f32),
            states,
            states,
            pltpu.VMEM((total * heads, wide), f32),
            pltpu.SemaphoreType.DMA((3,)),
            pltpu.SemaphoreType.DMA((3, sources)),
            pltpu.SemaphoreType.DMA,
            pltpu.SemaphoreType.DMA((sources,)),
            pltpu.SemaphoreType.DMA((3,)),
            pltpu.SemaphoreType.DMA((3,)),
            pltpu.SemaphoreType.DMA,
        ],
        compiler_params=pltpu.CompilerParams(
            collective_id=0, has_side_effects=True, vmem_limit_bytes=56 << 20
        ),
        name="lightning",
    )(doc_lengths, queries, key_vectors, value_vectors, jnp.transpose(log_decay, (1, 2, 0)))


def solution(mesh):
    return jax.shard_map(
        functools.partial(per_device, mesh.shape["ctx"]),
        mesh=mesh,
        in_specs=(
            P(("ctx", "head"), None, None, None),
            P(("ctx", "head"), None, None, None),
            P(("ctx", "head"), None, None, None),
            P(("ctx", "head"), None, None),
            P(),
        ),
        out_specs=P("ctx", "head", None),
        check_vma=False,
    )
```

```python
import functools

import jax
import jax.numpy as jnp
from jax import lax
from jax.experimental import pallas as pl
from jax.experimental.pallas import tpu as pltpu
from jax.sharding import PartitionSpec as P

EPSILON = 1e-06
SIDE = 4
BLOCKED = -1e30
EXACT = lax.Precision.HIGHEST
MESH = pl.DeviceIdType.MESH

MIXED = (10, 1, 6, 3, 9, 4, 14, 12, 11, 5, 2, 15, 8, 7, 13)
GROUPS = ((1, 3, 4, 12), (5, 15, 7, 13), (2, 8), (6, 14, 9, 11), (10,))
USED = (0,) + sum(GROUPS, ())


def packed(offsets):
    code = sum(off << (4 * n) for n, off in enumerate(offsets))
    return code - (1 << 32) if code >= 1 << 31 else code


FIRST_CODES, LAST_CODES = packed(USED[:8]), packed(USED[8:])


def split(x):
    high = x.astype(jnp.bfloat16)
    return high, (x - high.astype(jnp.float32)).astype(jnp.bfloat16)


def twice(high, low):
    row = jnp.concatenate([high, low], axis=1)
    return jnp.concatenate([row, row], axis=0)


def stacked(high, low):
    return jnp.concatenate(
        [jnp.concatenate([high, high], axis=1), jnp.concatenate([low, low], axis=1)],
        axis=0,
    )


def halves(x):
    half = x.shape[1] // 2
    return x[:, :half] + x[:, half:]


def product(left, right):
    return halves(jnp.dot(left, right, preferred_element_type=jnp.float32))


def product_t(left, right):
    return halves(
        lax.dot_general(
            left, right, (((1,), (1,)), ((), ())), preferred_element_type=jnp.float32
        )
    )


def kernel(
    tokens, heads, n_ctx,
    docs_in, q, k, v, gates, out,
    land_kv, land_q, gate_in, keep, tail, carry, step, update,
    k_high, k_low, v_high, v_low, s_high, s_low, own_state, near_states, near_sum, far_sum, docs, docs_sem,
    kv_send, kv_recv, q_send, q_recv, gate_send, gate_recv, state_send, state_recv,
):
    sources = SIDE * SIDE
    wide = 128
    ctx = lax.axis_index("ctx")
    me = lax.axis_index("head")
    x, y = me // SIDE, me % SIDE

    def to(off):
        return (x + off // SIDE) % SIDE * SIDE + (y + off % SIDE) % SIDE

    def source(n):
        codes = jnp.where(n < 8, FIRST_CODES, LAST_CODES)
        off = lax.shift_right_arithmetic(codes, 4 * (n % 8)) % 16
        return (x + SIDE - off // SIDE) % SIDE * SIDE + (y + SIDE - off % SIDE) % SIDE

    pltpu.make_async_copy(docs_in, docs, docs_sem).start()
    for j in range(heads):
        for a, array in enumerate((k, v)):
            pltpu.make_async_copy(
                array.at[:, me, j], land_kv.at[j, me, a], kv_recv.at[j, me]
            ).start()
        pltpu.make_async_copy(q.at[:, me, j], land_q.at[j, me], q_recv.at[j, me]).start()
    pltpu.make_async_copy(gates.at[me], gate_in.at[me], gate_recv.at[me]).start()

    barrier = pltpu.get_barrier_semaphore()
    for off in range(1, sources):
        pl.semaphore_signal(barrier, inc=1, device_id={"head": to(off)}, device_id_type=MESH)
    for hop in (1, 2, n_ctx - 1, n_ctx - 2):
        pl.semaphore_signal(
            barrier, inc=1, device_id={"ctx": (ctx + hop) % n_ctx}, device_id_type=MESH
        )
    pl.semaphore_wait(barrier, sources + 3)

    def send(source_ref, target_ref, send_sem, recv_sem, off):
        pltpu.make_async_remote_copy(
            src_ref=source_ref, dst_ref=target_ref, send_sem=send_sem, recv_sem=recv_sem,
            device_id={"head": to(off)}, device_id_type=MESH,
        ).start()

    for off in MIXED:
        send(gates.at[to(off)], gate_in.at[me], gate_send, gate_recv.at[me], off)
    for a, array in enumerate((k, v)):
        for j in range(heads):
            for off in MIXED:
                send(array.at[:, to(off), j], land_kv.at[j, me, a], kv_send.at[a], kv_recv.at[j, me], off)
    for group in GROUPS:
        for j in range(heads):
            for off in group:
                send(q.at[:, to(off), j], land_q.at[j, me], q_send, q_recv.at[j, me], off)

    for ref in (k_high, k_low, v_high, v_low):

        def clear(s, _, ref=ref):
            for j in range(heads):
                ref[j, s, tokens:, :] = jnp.zeros((wide - tokens, wide), jnp.bfloat16)
            return 0

        lax.fori_loop(0, sources, clear, 0)
    pltpu.make_async_copy(docs_in, docs, docs_sem).wait()
    ends = []
    for d in range(docs.shape[0]):
        ends.append(docs[d] + (ends[-1] if ends else 0))

    def doc_of(position):
        return sum((end <= position).astype(jnp.int32) for end in ends)

    row = lax.broadcasted_iota(jnp.int32, (tokens, wide), 0)
    col = lax.broadcasted_iota(jnp.int32, (tokens, wide), 1)
    upto_col = (row <= col).astype(jnp.float32)
    upto_row = (row >= col).astype(jnp.float32)[:, :tokens]

    def weigh(s, _):
        pltpu.make_async_copy(gate_in.at[s], gate_in.at[s], gate_recv.at[s]).wait()
        gate = gate_in[s]
        along_row = jnp.dot(gate, upto_col, precision=EXACT, preferred_element_type=jnp.float32)
        along_col = lax.dot_general(
            upto_row, gate, (((1,), (1,)), ((), ())), precision=EXACT, preferred_element_type=jnp.float32
        )
        start = (ctx * sources + s) * tokens
        doc_col = doc_of(start + row)
        doc_row = doc_of(start + col[:1])
        before = jnp.full((1, wide), start - 1, jnp.int32)
        doc_before = jnp.where(before >= 0, doc_of(before), -1)
        doc_last = doc_of(before + tokens)
        seen = (row >= col) & (doc_col == doc_row)
        same_first = doc_col == doc_before
        same_last = doc_col == doc_last
        for j in range(heads):
            col_sum = jnp.broadcast_to(along_col[:, j : j + 1], (tokens, wide))
            row_sum = along_row[j : j + 1, :]
            last = along_row[j : j + 1, tokens - 1 : tokens]
            keep[j, s] = jnp.exp(jnp.where(seen, col_sum - row_sum, BLOCKED))
            tail[j, s] = jnp.exp(jnp.where(same_last, last - col_sum, BLOCKED))
            through = jnp.exp(jnp.where(same_first, col_sum, BLOCKED))
            carry[j, s] = through
            step[j, s] = jnp.broadcast_to(through[tokens - 1 :, :], (8, wide))
        return 0

    lax.fori_loop(0, sources, weigh, 0)

    filler = jnp.zeros((wide - tokens, wide), jnp.float32)

    def gather(j, s):
        keys = land_kv[j, s, 0]
        values = land_kv[j, s, 1]
        k_high[j, s, :tokens, :], k_low[j, s, :tokens, :] = split(keys)
        v_high[j, s, :tokens, :], v_low[j, s, :tokens, :] = split(values)
        weighted = jnp.concatenate([keys * tail[j, s], filler], axis=0)
        flipped = jnp.concatenate([values, filler], axis=0).T
        update[j, s] = product(
            jnp.concatenate(split(flipped), axis=1), twice(*split(weighted))
        )

    def hand_on(source_ref, target_ref, n, j, hop):
        return pltpu.make_async_remote_copy(
            src_ref=source_ref.at[j], dst_ref=target_ref.at[j],
            send_sem=state_send.at[n, j], recv_sem=state_recv.at[n, j],
            device_id={"ctx": (ctx + hop) % n_ctx}, device_id_type=MESH,
        )

    def by_one(j):
        return hand_on(own_state, near_states.at[0], 0, j, 1)

    def by_two(j):
        return hand_on(own_state, near_states.at[1], 1, j, 2)

    def sums(j):
        return hand_on(near_sum, far_sum, 2, j, 2)

    def close(j):
        def onward(s, running):
            state, factor = running
            return step[j, s, :1, :] * state + update[j, s], step[j, s] * factor

        state, factor = lax.fori_loop(
            0, sources, onward, (jnp.zeros((wide, wide), jnp.float32), jnp.ones((8, wide), jnp.float32))
        )
        own_state[j, :wide, :] = state
        own_state[j, wide:, :] = factor
        by_two(j).start()
        by_one(j).start()

    def join(j):
        by_one(j).wait_recv()
        by_two(j).wait_recv()
        near_sum[j] = near_states[0, j, :wide, :] + near_states[0, j, wide : wide + 1, :] * near_states[1, j, :wide, :]
        sums(j).start()

    def enter(j):
        sums(j).wait_recv()
        both = near_states[0, j, wide : wide + 1, :] * near_states[1, j, wide : wide + 1, :]

        def onward(s, state):
            s_high[j, s], s_low[j, s] = split(state)
            return step[j, s, :1, :] * state + update[j, s]

        lax.fori_loop(0, sources, onward, near_sum[j] + both * far_sum[j])

    rows_out = out.reshape(sources * tokens * heads, wide)

    def answer(j, s):
        queries = jnp.concatenate(split(land_q[j, s]), axis=1)
        scores = product_t(queries, stacked(k_high[j, s], k_low[j, s]))
        carried = product_t(queries, stacked(s_high[j, s], s_low[j, s]))
        weights = jnp.concatenate(split(scores * keep[j, s]), axis=1)
        mixed = product(weights, twice(v_high[j, s], v_low[j, s])) + carry[j, s] * carried
        size = jnp.mean(mixed * mixed, axis=1, keepdims=True)
        rows_out[pl.ds(s * (tokens * heads) + j, tokens, stride=heads), :] = mixed * lax.rsqrt(size + EPSILON)

    def over_sources(work, land, recv_sem):
        def one(n, _):
            s = source(n)
            for j in range(heads):
                pltpu.make_async_copy(land.at[j, s], land.at[j, s], recv_sem.at[j, s]).wait()
            for j in range(heads):
                work(j, s)
            return 0

        lax.fori_loop(0, sources, one, 0)

    over_sources(gather, land_kv, kv_recv)
    for j in range(heads):
        close(j)
    for j in range(heads):
        join(j)
    for j in range(heads):
        enter(j)
    over_sources(answer, land_q, q_recv)

    for j in range(heads):
        by_one(j).wait_send()
        by_two(j).wait_send()
        sums(j).wait_send()
    others = pl.ds(0, sources - 1)
    pltpu.make_async_copy(gates.at[others], gates.at[others], gate_send).wait()
    for array, sem in ((k, kv_send.at[0]), (v, kv_send.at[1]), (q, q_send)):
        pltpu.make_async_copy(array.at[:, others], array.at[:, others], sem).wait()


def per_device(n_ctx, queries, key_vectors, value_vectors, log_decay, doc_lengths):
    tokens, sources, heads, wide = queries.shape
    f32 = jnp.float32
    hbm = pl.BlockSpec(memory_space=pltpu.HBM)
    per_block = (heads, sources)
    block = pltpu.VMEM((*per_block, tokens, wide), f32)
    square = pltpu.VMEM((*per_block, wide, wide), jnp.bfloat16)
    states = pltpu.VMEM((heads, wide, wide), f32)
    dma = pltpu.SemaphoreType.DMA

    def stays(array):
        return pltpu.with_memory_space_constraint(array, pltpu.HBM)

    return pl.pallas_call(
        functools.partial(kernel, tokens, heads, n_ctx),
        out_shape=jax.ShapeDtypeStruct((sources * tokens, heads, wide), f32),
        in_specs=[hbm] * 5,
        out_specs=pl.BlockSpec(memory_space=pltpu.VMEM),
        scratch_shapes=[
            pltpu.VMEM((*per_block, 2, tokens, wide), f32),
            block,
            pltpu.VMEM((sources, heads, tokens), f32),
            block,
            block,
            block,
            pltpu.VMEM((*per_block, 8, wide), f32),
            pltpu.VMEM((*per_block, wide, wide), f32),
            *[square] * 6,
            pltpu.VMEM((heads, wide + 8, wide), f32),
            pltpu.VMEM((2, heads, wide + 8, wide), f32),
            states,
            states,
            pltpu.SMEM(doc_lengths.shape, jnp.int32),
            dma,
            dma((2,)),
            dma(per_block),
            dma,
            dma(per_block),
            dma,
            dma((sources,)),
            dma((3, heads)),
            dma((3, heads)),
        ],
        compiler_params=pltpu.CompilerParams(
            collective_id=0, has_side_effects=True, vmem_limit_bytes=48 << 20
        ),
        name="lightning",
    )(
        stays(doc_lengths), queries, key_vectors, value_vectors, stays(jnp.transpose(log_decay, (1, 2, 0)))
    )


def solution(mesh):
    return jax.shard_map(
        functools.partial(per_device, mesh.shape["ctx"]),
        mesh=mesh,
        in_specs=(
            P(("ctx", "head"), None, None, None),
            P(("ctx", "head"), None, None, None),
            P(("ctx", "head"), None, None, None),
            P(("ctx", "head"), None, None),
            P(),
        ),
        out_specs=P("ctx", "head", None),
        check_vma=False,
    )
```

```python
import functools

import jax
import jax.numpy as jnp
from jax import lax
from jax.experimental import pallas as pl
from jax.experimental.pallas import tpu as pltpu
from jax.sharding import PartitionSpec as P

EPSILON = 1e-06
SIDE = 4
BLOCKED = -1e30
EXACT = lax.Precision.HIGHEST
MESH = pl.DeviceIdType.MESH

MIXED = (10, 1, 6, 3, 9, 4, 14, 12, 11, 5, 2, 15, 8, 7, 13)
GROUPS = ((1, 3, 4, 12), (5, 15, 7, 13), (2, 8), (6, 14, 9, 11), (10,))
USED = (0,) + sum(GROUPS, ())


def packed(offsets):
    code = sum(off << (4 * n) for n, off in enumerate(offsets))
    return code - (1 << 32) if code >= 1 << 31 else code


FIRST_CODES, LAST_CODES = packed(USED[:8]), packed(USED[8:])


def split(x):
    high = x.astype(jnp.bfloat16)
    return high, (x - high.astype(jnp.float32)).astype(jnp.bfloat16)


def twice(high, low):
    row = jnp.concatenate([high, low], axis=1)
    return jnp.concatenate([row, row], axis=0)


def stacked(high, low):
    return jnp.concatenate(
        [jnp.concatenate([high, high], axis=1), jnp.concatenate([low, low], axis=1)],
        axis=0,
    )


def halves(x):
    half = x.shape[1] // 2
    return x[:, :half] + x[:, half:]


def product(left, right):
    return halves(jnp.dot(left, right, preferred_element_type=jnp.float32))


def product_t(left, right):
    return halves(
        lax.dot_general(
            left, right, (((1,), (1,)), ((), ())), preferred_element_type=jnp.float32
        )
    )


def kernel(
    tokens, heads, n_ctx,
    docs_in, q, k, v, gates, out,
    land_kv, land_q, gate_in, keep, tail, carry, step, update,
    k_high, k_low, v_high, v_low, s_high, s_low, own_state, near_states, near_sum, far_sum, docs, docs_sem,
    kv_send, kv_recv, q_send, q_recv, gate_send, gate_recv, state_send, state_recv,
):
    sources = SIDE * SIDE
    wide = 128
    ctx = lax.axis_index("ctx")
    me = lax.axis_index("head")
    x, y = me // SIDE, me % SIDE

    rows_of = [(x + d) % SIDE * SIDE for d in range(SIDE)]
    columns_of = [(y + d) % SIDE for d in range(SIDE)]
    places = [a + b for a in rows_of for b in columns_of]

    def to(off):
        return places[off]

    def source(n):
        codes = jnp.where(n < 8, FIRST_CODES, LAST_CODES)
        off = lax.shift_right_arithmetic(codes, 4 * (n % 8)) % 16
        return (x + SIDE - off // SIDE) % SIDE * SIDE + (y + SIDE - off % SIDE) % SIDE

    barrier = pltpu.get_barrier_semaphore()
    for off in range(1, sources):
        pl.semaphore_signal(barrier, inc=1, device_id={"head": to(off)}, device_id_type=MESH)
    for hop in (1, 2, n_ctx - 1, n_ctx - 2):
        pl.semaphore_signal(
            barrier, inc=1, device_id={"ctx": (ctx + hop) % n_ctx}, device_id_type=MESH
        )
    pltpu.make_async_copy(docs_in, docs, docs_sem).start()
    for j in range(heads):
        for a, array in enumerate((k, v)):
            pltpu.make_async_copy(
                array.at[:, me, j], land_kv.at[j, me, a], kv_recv.at[j, me]
            ).start()
        pltpu.make_async_copy(q.at[:, me, j], land_q.at[j, me], q_recv.at[j, me]).start()
    pltpu.make_async_copy(gates.at[me], gate_in.at[me], gate_recv.at[me]).start()

    pl.semaphore_wait(barrier, sources + 3)

    def send(source_ref, target_ref, send_sem, recv_sem, off):
        pltpu.make_async_remote_copy(
            src_ref=source_ref, dst_ref=target_ref, send_sem=send_sem, recv_sem=recv_sem,
            device_id={"head": to(off)}, device_id_type=MESH,
        ).start()

    for a, array in enumerate((k, v)):
        for j in range(heads):
            for off in MIXED:
                send(array.at[:, to(off), j], land_kv.at[j, me, a], kv_send.at[a], kv_recv.at[j, me], off)
                if j == a == 0:
                    send(gates.at[to(off)], gate_in.at[me], gate_send, gate_recv.at[me], off)
    for group in GROUPS:
        for j in range(heads):
            for off in group:
                send(q.at[:, to(off), j], land_q.at[j, me], q_send, q_recv.at[j, me], off)

    for ref in (k_high, k_low, v_high, v_low):

        def clear(s, _, ref=ref):
            for j in range(heads):
                ref[j, s, tokens:, :] = jnp.zeros((wide - tokens, wide), jnp.bfloat16)
            return 0

        lax.fori_loop(0, sources, clear, 0)
    pltpu.make_async_copy(docs_in, docs, docs_sem).wait()
    ends = []
    for d in range(docs.shape[0]):
        ends.append(docs[d] + (ends[-1] if ends else 0))

    def doc_of(position):
        return sum((end <= position).astype(jnp.int32) for end in ends)

    row = lax.broadcasted_iota(jnp.int32, (tokens, wide), 0)
    col = lax.broadcasted_iota(jnp.int32, (tokens, wide), 1)
    upto_col = (row <= col).astype(jnp.float32)
    upto_row = (row >= col).astype(jnp.float32)[:, :tokens]

    def weigh(s, _):
        pltpu.make_async_copy(gate_in.at[s], gate_in.at[s], gate_recv.at[s]).wait()
        gate = gate_in[s]
        along_row = jnp.dot(gate, upto_col, precision=EXACT, preferred_element_type=jnp.float32)
        along_col = lax.dot_general(
            upto_row, gate, (((1,), (1,)), ((), ())), precision=EXACT, preferred_element_type=jnp.float32
        )
        start = (ctx * sources + s) * tokens
        doc_col = doc_of(start + row)
        doc_row = doc_of(start + col[:1])
        before = jnp.full((1, wide), start - 1, jnp.int32)
        doc_before = jnp.where(before >= 0, doc_of(before), -1)
        doc_last = doc_of(before + tokens)
        seen = (row >= col) & (doc_col == doc_row)
        same_first = doc_col == doc_before
        same_last = doc_col == doc_last
        for j in range(heads):
            col_sum = jnp.broadcast_to(along_col[:, j : j + 1], (tokens, wide))
            row_sum = along_row[j : j + 1, :]
            last = along_row[j : j + 1, tokens - 1 : tokens]
            keep[j, s] = jnp.exp(jnp.where(seen, col_sum - row_sum, BLOCKED))
            tail[j, s] = jnp.exp(jnp.where(same_last, last - col_sum, BLOCKED))
            through = jnp.exp(jnp.where(same_first, col_sum, BLOCKED))
            carry[j, s] = through
            step[j, s] = jnp.broadcast_to(through[tokens - 1 :, :], (8, wide))
        return 0

    lax.fori_loop(0, sources, weigh, 0)

    filler = jnp.zeros((wide - tokens, wide), jnp.float32)

    def gather(j, s):
        keys = land_kv[j, s, 0]
        values = land_kv[j, s, 1]
        k_high[j, s, :tokens, :], k_low[j, s, :tokens, :] = split(keys)
        v_high[j, s, :tokens, :], v_low[j, s, :tokens, :] = split(values)
        weighted = jnp.concatenate([keys * tail[j, s], filler], axis=0)
        flipped = jnp.concatenate([values, filler], axis=0).T
        update[j, s] = product(
            jnp.concatenate(split(flipped), axis=1), twice(*split(weighted))
        )

    def hand_on(source_ref, target_ref, n, j, hop):
        return pltpu.make_async_remote_copy(
            src_ref=source_ref.at[j], dst_ref=target_ref.at[j],
            send_sem=state_send.at[n, j], recv_sem=state_recv.at[n, j],
            device_id={"ctx": (ctx + hop) % n_ctx}, device_id_type=MESH,
        )

    def by_one(j):
        return hand_on(own_state, near_states.at[0], 0, j, 1)

    def by_two(j):
        return hand_on(own_state, near_states.at[1], 1, j, 2)

    def sums(j):
        return hand_on(near_sum, far_sum, 2, j, 2)

    def close(j):
        def onward(s, running):
            state, factor = running
            return step[j, s, :1, :] * state + update[j, s], step[j, s] * factor

        state, factor = lax.fori_loop(
            0, sources, onward, (jnp.zeros((wide, wide), jnp.float32), jnp.ones((8, wide), jnp.float32))
        )
        own_state[j, :wide, :] = state
        own_state[j, wide:, :] = factor
        by_two(j).start()
        by_one(j).start()

    def join(j):
        by_one(j).wait_recv()
        by_two(j).wait_recv()
        near_sum[j] = near_states[0, j, :wide, :] + near_states[0, j, wide : wide + 1, :] * near_states[1, j, :wide, :]
        sums(j).start()

    def enter(j):
        sums(j).wait_recv()
        both = near_states[0, j, wide : wide + 1, :] * near_states[1, j, wide : wide + 1, :]

        def onward(s, state):
            s_high[j, s], s_low[j, s] = split(state)
            return step[j, s, :1, :] * state + update[j, s]

        lax.fori_loop(0, sources, onward, near_sum[j] + both * far_sum[j])

    rows_out = out.reshape(sources * tokens * heads, wide)

    def answer(j, s):
        queries = jnp.concatenate(split(land_q[j, s]), axis=1)
        scores = product_t(queries, stacked(k_high[j, s], k_low[j, s]))
        carried = product_t(queries, stacked(s_high[j, s], s_low[j, s]))
        weights = jnp.concatenate(split(scores * keep[j, s]), axis=1)
        mixed = product(weights, twice(v_high[j, s], v_low[j, s])) + carry[j, s] * carried
        size = jnp.mean(mixed * mixed, axis=1, keepdims=True)
        rows_out[pl.ds(s * (tokens * heads) + j, tokens, stride=heads), :] = mixed * lax.rsqrt(size + EPSILON)

    def over_sources(work, land, recv_sem):
        def one(n, _):
            s = source(n)
            for j in range(heads):
                pltpu.make_async_copy(land.at[j, s], land.at[j, s], recv_sem.at[j, s]).wait()
            for j in range(heads):
                work(j, s)
            return 0

        lax.fori_loop(0, sources, one, 0)

    over_sources(gather, land_kv, kv_recv)
    for j in range(heads):
        close(j)
    for j in range(heads):
        join(j)
    for j in range(heads):
        enter(j)
    over_sources(answer, land_q, q_recv)

    for j in range(heads):
        by_one(j).wait_send()
        by_two(j).wait_send()
        sums(j).wait_send()
    others = pl.ds(0, sources - 1)
    pltpu.make_async_copy(gates.at[others], gates.at[others], gate_send).wait()
    for array, sem in ((k, kv_send.at[0]), (v, kv_send.at[1]), (q, q_send)):
        pltpu.make_async_copy(array.at[:, others], array.at[:, others], sem).wait()


def per_device(n_ctx, queries, key_vectors, value_vectors, log_decay, doc_lengths):
    tokens, sources, heads, wide = queries.shape
    f32 = jnp.float32
    hbm = pl.BlockSpec(memory_space=pltpu.HBM)
    per_block = (heads, sources)
    block = pltpu.VMEM((*per_block, tokens, wide), f32)
    square = pltpu.VMEM((*per_block, wide, wide), jnp.bfloat16)
    states = pltpu.VMEM((heads, wide, wide), f32)
    dma = pltpu.SemaphoreType.DMA

    def stays(array):
        return pltpu.with_memory_space_constraint(array, pltpu.HBM)

    return pl.pallas_call(
        functools.partial(kernel, tokens, heads, n_ctx),
        out_shape=jax.ShapeDtypeStruct((sources * tokens, heads, wide), f32),
        in_specs=[hbm] * 5,
        out_specs=pl.BlockSpec(memory_space=pltpu.VMEM),
        scratch_shapes=[
            pltpu.VMEM((*per_block, 2, tokens, wide), f32),
            block,
            pltpu.VMEM((sources, heads, tokens), f32),
            block,
            block,
            block,
            pltpu.VMEM((*per_block, 8, wide), f32),
            pltpu.VMEM((*per_block, wide, wide), f32),
            *[square] * 6,
            pltpu.VMEM((heads, wide + 8, wide), f32),
            pltpu.VMEM((2, heads, wide + 8, wide), f32),
            states,
            states,
            pltpu.SMEM(doc_lengths.shape, jnp.int32),
            dma,
            dma((2,)),
            dma(per_block),
            dma,
            dma(per_block),
            dma,
            dma((sources,)),
            dma((3, heads)),
            dma((3, heads)),
        ],
        compiler_params=pltpu.CompilerParams(
            collective_id=0, has_side_effects=True, vmem_limit_bytes=48 << 20
        ),
        name="lightning",
    )(
        stays(doc_lengths), queries, key_vectors, value_vectors, stays(jnp.transpose(log_decay, (1, 2, 0)))
    )


def solution(mesh):
    return jax.shard_map(
        functools.partial(per_device, mesh.shape["ctx"]),
        mesh=mesh,
        in_specs=(
            P(("ctx", "head"), None, None, None),
            P(("ctx", "head"), None, None, None),
            P(("ctx", "head"), None, None, None),
            P(("ctx", "head"), None, None),
            P(),
        ),
        out_specs=P("ctx", "head", None),
        check_vma=False,
    )
```
